32 devices in a mesh: groups: 2 (over y), tiles: 16 (over z, x, core).
Axes of the slice: x: 2, y: 2, z: 4, core: 2. Of those that a mesh axis runs over, the one named last changes fastest.
Arguments:
- raw: bfloat16 [16, 256, 2048], P(None, ('groups', 'tiles')), parts along dimension 1, may hold values from -40 to 40, as said below
- fir: float32 [64], replicated, may hold values from -0.75 to 0.75
- keep: int32 [16, 256], P(None, ('groups', 'tiles')), parts along dimension 1, may hold values 0 or 1
- table: int32 [16, 2], replicated, may hold values from 0 to 0, as said below
Outputs:
- stacks: bfloat16 [32, 128, 128, 256], P(('groups', 'tiles')), parts along dimension 0
The draws below stay inside these ranges and needn't reach their ends.
There are 2 independent parts, one for each index of `groups`. The reference program is written for one: setup_inputs(seed, part) draws one part's arguments, and reference() takes and returns one part's arrays. A program takes and returns all parts, laid end to end along the dimension named above; an argument that names none is the same for every part. Nothing has to cross between parts.
Inputs may be any that keep to these rules, and one draw needn't show every extreme that they name: `table`: each row holds r <= c. `raw`: a common motion of all channels plus independent noise.
All inputs are finite; a program needn't handle non-finite values. No bound on the sum of `keep` on one device may be relied on, other than what follows from the above.
Results may differ from the reference program's by a relative error of at most 0.0053.
Values may be sent and summed in bfloat16 or wider, within the bound.
A program may use at most 128 MiB of HBM per device.

```python
import jax
import jax.numpy as jnp
from jax import lax

WINDOWS = 16
TILE = 128
SEG = 512
LAGS = 256
TAPS = 64
DEC = 4
RAW = 2048
NBIN = 256
CHANNELS = 128
BLOCKS = 1
N_TILES = 16


def draw_raw(key, part):
    noise_key = jax.random.fold_in(key, 11)
    common_key = jax.random.fold_in(key, 12)
    gain_key = jax.random.fold_in(key, 13)
    noise = jax.random.normal(noise_key, (WINDOWS, CHANNELS, RAW), jnp.float32)
    common = jax.random.normal(common_key, (WINDOWS, 1, RAW), jnp.float32)
    gain = jnp.exp(jax.random.uniform(gain_key, (1, CHANNELS, 1), jnp.float32, -0.7, 0.7))
    return jnp.clip(noise + 2.0 * gain * common, -40.0, 40.0).astype(jnp.bfloat16)


def draw_table(key, part):
    pair = jax.random.randint(jax.random.fold_in(key, 21), (N_TILES, 2), 0, BLOCKS)
    low = jnp.minimum(pair[:, 0], pair[:, 1])
    high = jnp.maximum(pair[:, 0], pair[:, 1])
    high = high.at[0].set(BLOCKS - 1)
    return jnp.stack([low, high], 1).astype(jnp.int32)


def touch_ends(drawn, own_key, low, largest):
    place = [jax.random.randint(jax.random.fold_in(own_key, axis), (), 0, length) for axis, length in enumerate(drawn.shape)]
    widest = drawn.shape.index(max(drawn.shape))
    neighbour = place[:widest] + [(place[widest] + 1) % drawn.shape[widest]] + place[widest + 1:]
    return drawn.at[tuple(place)].set(low).at[tuple(neighbour)].set(largest)


def gaussian(own_key, shape, spread, reach, kind=jnp.bfloat16):
    return jnp.clip(spread * jax.random.normal(own_key, shape, jnp.float32), -reach, reach).astype(kind)


def setup_inputs(seed: int = 0, part: int = 0) -> dict:
    keys = jax.random.split(jax.random.key(seed), 5)
    part_splits = jax.random.split(jax.random.fold_in(keys[4], part), 5)
    raw = draw_raw(jax.random.fold_in(jax.random.fold_in(keys[4], part), 71), part)
    fir = gaussian(keys[1], (TAPS,), TAPS ** -0.5, 0.75, jnp.float32)
    keep = touch_ends((jax.random.randint(part_splits[2], (WINDOWS, CHANNELS), 0, 8) < 7).astype(jnp.int32), jax.random.fold_in(part_splits[2], 1), 0, 1)
    table = draw_table(jax.random.fold_in(keys[4], 71), part)
    return dict(raw=raw, fir=fir, keep=keep, table=table)


def filter_band(fir):
    period = 2 * RAW + TAPS
    pattern = jnp.concatenate([fir[:1], jnp.zeros((period - TAPS,), jnp.float32), fir[1:][::-1]])
    tiled = jnp.tile(pattern, SEG)[:SEG * (period - DEC)].reshape(SEG, period - DEC)
    return tiled[:, :RAW]

def filter_block(raw, fir):
    band = filter_band(fir)
    return jnp.einsum('wcm,nm->wcn', raw.astype(jnp.float32), band, precision=lax.Precision.HIGHEST)

def dft_tables():
    steps = jnp.arange(SEG, dtype=jnp.int32)
    freqs = jnp.arange(NBIN, dtype=jnp.int32)
    angle = 2.0 * jnp.pi / SEG * jnp.mod(steps[:, None] * freqs[None, :], SEG).astype(jnp.float32)
    return (jnp.cos(angle), jnp.sin(angle))

def whiten(decimated, keep):
    cosine, sine = dft_tables()
    real_part = jnp.einsum('wcn,nf->wcf', decimated, cosine, precision=lax.Precision.HIGHEST)
    imag_part = -jnp.einsum('wcn,nf->wcf', decimated, sine, precision=lax.Precision.HIGHEST)
    power = real_part * real_part + imag_part * imag_part
    level = lax.optimization_barrier(jnp.mean(power, -1, keepdims=True))
    scale = keep.astype(jnp.float32)[..., None] / jnp.sqrt(0.5 * power + 0.5 * level + 1e-05)
    return jnp.concatenate([real_part * scale, imag_part * scale], -1).astype(jnp.bfloat16)

def cross_tile(rows, cols):
    half = rows.shape[-1] // 2
    row_re, row_im = (rows[..., :half], rows[..., half:])
    col_re, col_im = (cols[..., :half], cols[..., half:])
    cross_re = jnp.einsum('wif,wjf->ijf', row_re, col_re, preferred_element_type=jnp.float32)
    cross_re = cross_re + jnp.einsum('wif,wjf->ijf', row_im, col_im, preferred_element_type=jnp.float32)
    cross_im = jnp.einsum('wif,wjf->ijf', row_re, col_im, preferred_element_type=jnp.float32)
    cross_im = cross_im - jnp.einsum('wif,wjf->ijf', row_im, col_re, preferred_element_type=jnp.float32)
    return jnp.concatenate([cross_re, cross_im], -1).astype(jnp.bfloat16)

def lag_table():
    freqs = jnp.arange(NBIN, dtype=jnp.int32)
    shifts = jnp.arange(LAGS, dtype=jnp.int32) - LAGS // 2
    angle = 2.0 * jnp.pi / SEG * jnp.mod(freqs[:, None] * shifts[None, :], SEG).astype(jnp.float32)
    weight = jnp.where(freqs == 0, 1.0, 2.0).astype(jnp.float32)[:, None] / jnp.sqrt(jnp.float32(WINDOWS * NBIN))
    return jnp.concatenate([weight * jnp.cos(angle), -weight * jnp.sin(angle)], 0).astype(jnp.bfloat16)

def reference(raw, fir, keep, table):
    filtered = filter_block(raw, fir)
    common = lax.optimization_barrier(jnp.mean(filtered, 1, keepdims=True))
    whitened = whiten(filtered - common, keep)
    lags = lag_table()

    def one_tile(entry):
        rows = lax.dynamic_slice_in_dim(whitened, (entry[0] * TILE).astype(jnp.int32), TILE, 1)
        cols = lax.dynamic_slice_in_dim(whitened, (entry[1] * TILE).astype(jnp.int32), TILE, 1)
        cross = cross_tile(rows, cols).reshape(TILE * TILE, 2 * NBIN)
        return jnp.dot(cross, lags, preferred_element_type=jnp.float32).astype(jnp.bfloat16).reshape(TILE, TILE, LAGS)
    return lax.map(one_tile, table)
```

```python
import functools

import jax
import jax.numpy as jnp
import numpy as np
from jax import lax
from jax.experimental import pallas as pl
from jax.experimental.pallas import tpu as pltpu
from jax.sharding import PartitionSpec as P

WINDOWS = 16
TILE = 128
SEG = 512
LAGS = 256
TAPS = 64
DEC = 4
RAW = 2048
NBIN = 256
SPAN = 640
STRIDE = 520


def split2(x):
    high = x.astype(jnp.bfloat16)
    return high, (x - high.astype(jnp.float32)).astype(jnp.bfloat16)


def split3(x):
    high = x.astype(jnp.bfloat16)
    rest = x - high.astype(jnp.float32)
    middle = rest.astype(jnp.bfloat16)
    return high, middle, (rest - middle.astype(jnp.float32)).astype(jnp.bfloat16)


def contract(a, b, left, right):
    return lax.dot_general(a, b, (((left,), (right,)), ((), ())), preferred_element_type=jnp.float32)


def dft_tables():
    angle = 2.0 * np.pi / SEG * np.mod(np.arange(SEG)[:, None] * np.arange(NBIN)[None, :], SEG)
    table = np.concatenate([np.cos(angle), -np.sin(angle)], 1).astype(np.float32)
    high = table.astype(jnp.bfloat16)
    low = (table - high.astype(np.float32)).astype(jnp.bfloat16)
    return jnp.asarray(np.concatenate([high, low], 0))


def lag_table():
    freqs = np.arange(NBIN)
    shifts = np.arange(LAGS) - LAGS // 2
    angle = 2.0 * np.pi / SEG * np.mod(freqs[:, None] * shifts[None, :], SEG)
    weight = np.where(freqs == 0, 1.0, 2.0)[:, None] / np.sqrt(WINDOWS * NBIN)
    table = np.concatenate([weight * np.cos(angle), -weight * np.sin(angle)], 0)
    return jnp.asarray(table.astype(np.float32).astype(jnp.bfloat16))


def filter_rows(raw_ref, taps_ref):
    rows = raw_ref.shape[0] * raw_ref.shape[1]
    raw = raw_ref[...].astype(jnp.float32).reshape(rows, RAW).astype(jnp.bfloat16)
    band = jnp.broadcast_to(taps_ref[...], (TILE, SPAN))
    index = lax.broadcasted_iota(jnp.int32, (TILE, SPAN), 0)
    for bit in range(7):
        band = jnp.where((index >> bit) & 1 == 1, pltpu.roll(band, DEC << bit, 1), band)
    pieces = [jnp.concatenate([jnp.zeros((rows, TILE), jnp.bfloat16), raw[:, :SEG]], 1)]
    for block in range(1, RAW // SEG):
        pieces.append(raw[:, block * SEG - TILE : (block + 1) * SEG])
    spans = jnp.concatenate(pieces, 0)
    out = sum(contract(spans, part, 1, 1) for part in split3(band)[::-1])
    return jnp.concatenate([out[b * rows : (b + 1) * rows] for b in range(RAW // SEG)], 1)


def whiten_rows(decimated, keep, table_ref):
    high, low = split2(decimated)
    table_high = table_ref[:SEG, :]
    spectrum = contract(low, table_high, 1, 0) + contract(high, table_ref[SEG:, :], 1, 0)
    spectrum = spectrum + contract(high, table_high, 1, 0)
    real_part, imag_part = spectrum[:, :NBIN], spectrum[:, NBIN:]
    power = real_part * real_part + imag_part * imag_part
    level = jnp.mean(power, -1, keepdims=True)
    scale = keep.astype(jnp.float32) * lax.rsqrt(0.5 * power + 0.5 * level + 1e-05)
    return jnp.concatenate([real_part * scale, imag_part * scale], 1).astype(jnp.bfloat16)


def arrange(piece_ref, spectra_ref):
    members, rows = piece_ref.shape[:2]
    width = rows // WINDOWS
    for pair in range(WINDOWS // 2):
        for quarter in range(4):
            block = piece_ref[:, pair * 2 * width : (pair + 1) * 2 * width, quarter * 128 : (quarter + 1) * 128]
            block = block.astype(jnp.float32)
            for half in range(2):
                turned = block[:, half * width : (half + 1) * width].reshape(members * width, 128).T
                start = (quarter % 2) * 128 * 32 + (quarter // 2) * WINDOWS + pair * 2 + half
                spectra_ref[pl.ds(start, 128, 32), :] = turned


def stack_kernel(same, per_step, entry_ref, rows_ref, cols_ref, lag_ref, out_ref, row_spec, col_spec, cross_ref):
    @pl.when(pl.program_id(0) == 0)
    def _():
        arrange(rows_ref, row_spec)
        if not same:
            arrange(cols_ref, col_spec)

        def one_bin(f, carry):
            start = pl.multiple_of(f * 32, 32)
            left = row_spec[pl.ds(start, 32), :]
            right = left if same else col_spec[pl.ds(start, 32), :]
            turned = jnp.concatenate([right[WINDOWS:], -right[:WINDOWS]], 0)
            both = jnp.concatenate([right, turned], 1).astype(jnp.bfloat16)
            cross = contract(left.astype(jnp.bfloat16), both, 0, 0)
            cross_ref[pl.ds(f, TILE, STRIDE), :] = cross[:, :TILE]
            cross_ref[pl.ds(f + NBIN, TILE, STRIDE), :] = cross[:, TILE:]
            return carry

        lax.fori_loop(0, NBIN, one_bin, 0, unroll=8)

    base = pl.program_id(0) * per_step
    for group in range(per_step // 4):
        picked = []
        for member in range(4):
            start = pl.multiple_of((base + group * 4 + member) * STRIDE, 8)
            picked.append(cross_ref[pl.ds(start, 2 * NBIN), :].astype(jnp.bfloat16))
        stacked = contract(jnp.concatenate(picked, 1), lag_ref[...], 0, 0)
        out_ref[group * 4 : group * 4 + 4] = stacked.reshape(4, TILE, LAGS).astype(jnp.bfloat16)


def stack(gathered, entry):
    members = TILE * WINDOWS // gathered.shape[1]
    same = gathered.shape[0] == members
    per_step = 8
    block = (members,) + gathered.shape[1:]
    spec_shape = pltpu.VMEM((2 * NBIN * WINDOWS, TILE), jnp.float32)
    small = pltpu.VMEM((8, 128), jnp.float32)
    return pl.pallas_call(
        functools.partial(stack_kernel, same, per_step),
        out_shape=jax.ShapeDtypeStruct((TILE, TILE, LAGS), jnp.bfloat16),
        grid_spec=pltpu.PrefetchScalarGridSpec(
            num_scalar_prefetch=1,
            grid=(TILE // per_step,),
            in_specs=[
                pl.BlockSpec(block, lambda s, entry: (entry[0], 0, 0)),
                pl.BlockSpec((8, 128) if same else block, (lambda s, entry: (0, 0)) if same else (lambda s, entry: (entry[1], 0, 0))),
                pl.BlockSpec((2 * NBIN, LAGS), lambda s, entry: (0, 0)),
            ],
            out_specs=pl.BlockSpec((per_step, TILE, LAGS), lambda s, entry: (s, 0, 0)),
            scratch_shapes=[spec_shape, small if same else spec_shape, pltpu.VMEM((TILE * STRIDE, TILE), jnp.float32)],
        ),
        compiler_params=pltpu.CompilerParams(vmem_limit_bytes=60 << 20),
        cost_estimate=pl.CostEstimate(flops=10 << 30, bytes_accessed=12 << 20, transcendentals=0),
    )(entry, gathered, entry_dummy() if same else gathered, lag_table())


def entry_dummy():
    return jnp.zeros((8, 128), jnp.float32)


def taps_row(fir):
    return jnp.pad(fir[::-1], (TILE + 1 - TAPS, SPAN - TILE - 1))[None, :]


def filter_kernel(raw_ref, taps_ref, filtered_ref, sum_ref):
    filtered = filter_rows(raw_ref, taps_ref)
    filtered_ref[...] = filtered
    sum_ref[...] = jnp.sum(filtered.reshape(raw_ref.shape[0], raw_ref.shape[1], SEG), 1)


def whiten_kernel(channels, filtered_ref, sum_ref, keep_ref, table_ref, out_ref):
    rows = filtered_ref.shape[0]
    width = rows // WINDOWS
    common = sum_ref[...] / channels
    decimated = filtered_ref[...].reshape(WINDOWS, width, SEG) - common[:, None, :]
    out_ref[...] = whiten_rows(decimated.reshape(rows, SEG), keep_ref[...], table_ref)


def local(raw, fir, keep, table):
    devices = lax.axis_size("tiles")
    rows = raw.shape[0] * raw.shape[1]
    filtered, sums = pl.pallas_call(
        filter_kernel,
        out_shape=(jax.ShapeDtypeStruct((rows, SEG), jnp.float32), jax.ShapeDtypeStruct((WINDOWS, SEG), jnp.float32)),
        compiler_params=pltpu.CompilerParams(vmem_limit_bytes=32 << 20),
    )(raw, taps_row(fir))
    sums = lax.psum(sums, "tiles")
    whitened = pl.pallas_call(
        functools.partial(whiten_kernel, raw.shape[1] * devices),
        out_shape=jax.ShapeDtypeStruct((rows, 2 * NBIN), jnp.bfloat16),
        compiler_params=pltpu.CompilerParams(vmem_limit_bytes=32 << 20),
    )(filtered, sums, keep.reshape(rows, 1), dft_tables())
    gathered = lax.all_gather(whitened, "tiles", axis=0)
    entry = table[lax.axis_index("tiles")]
    return stack(gathered, entry)[None]


def solution(mesh):
    placed = (P(None, ("groups", "tiles"), None), P(), P(None, ("groups", "tiles")), P())
    return jax.shard_map(
        local,
        mesh=mesh,
        in_specs=placed,
        out_specs=P(("groups", "tiles"), None, None, None),
        check_vma=False,
    )
```

```python
import functools

import jax
import jax.numpy as jnp
import numpy as np
from jax import lax
from jax.experimental import pallas as pl
from jax.experimental.pallas import tpu as pltpu
from jax.sharding import PartitionSpec as P

WINDOWS = 16
TILE = 128
SEG = 512
LAGS = 256
TAPS = 64
DEC = 4
RAW = 2048
NBIN = 256
SPAN = 640
STRIDE = 520


def split2(x):
    high = x.astype(jnp.bfloat16)
    return high, (x - high.astype(jnp.float32)).astype(jnp.bfloat16)


def split3(x):
    high = x.astype(jnp.bfloat16)
    rest = x - high.astype(jnp.float32)
    middle = rest.astype(jnp.bfloat16)
    return high, middle, (rest - middle.astype(jnp.float32)).astype(jnp.bfloat16)


def contract(a, b, left, right):
    return lax.dot_general(a, b, (((left,), (right,)), ((), ())), preferred_element_type=jnp.float32)


def dft_tables():
    angle = 2.0 * np.pi / SEG * np.mod(np.arange(SEG)[:, None] * np.arange(NBIN)[None, :], SEG)
    table = np.concatenate([np.cos(angle), -np.sin(angle)], 1).astype(np.float32)
    high = table.astype(jnp.bfloat16)
    low = (table - high.astype(np.float32)).astype(jnp.bfloat16)
    return jnp.asarray(np.concatenate([high, low], 0))


def lag_table():
    freqs = np.arange(NBIN)
    shifts = np.arange(LAGS) - LAGS // 2
    angle = 2.0 * np.pi / SEG * np.mod(freqs[:, None] * shifts[None, :], SEG)
    weight = np.where(freqs == 0, 1.0, 2.0)[:, None] / np.sqrt(WINDOWS * NBIN)
    table = np.concatenate([weight * np.cos(angle), -weight * np.sin(angle)], 0)
    return jnp.asarray(table.astype(np.float32).astype(jnp.bfloat16))


def filter_rows(raw_ref, taps_ref):
    rows = raw_ref.shape[0] * raw_ref.shape[1]
    raw = raw_ref[...].astype(jnp.float32).reshape(rows, RAW).astype(jnp.bfloat16)
    taps = jnp.broadcast_to(taps_ref[...], (8, TAPS))
    places = lax.broadcasted_iota(jnp.int32, (TAPS, SPAN), 0) + lax.broadcasted_iota(jnp.int32, (TAPS, SPAN), 1)
    pick = jnp.where(places == TILE, 1.0, 0.0).astype(jnp.bfloat16)
    spread = sum(contract(part, pick, 1, 0) for part in split3(taps)[::-1])
    band = jnp.broadcast_to(spread[:1], (TILE, SPAN))
    index = lax.broadcasted_iota(jnp.int32, (TILE, SPAN), 0)
    for bit in range(7):
        band = jnp.where((index >> bit) & 1 == 1, pltpu.roll(band, DEC << bit, 1), band)
    pieces = [jnp.concatenate([jnp.zeros((rows, TILE), jnp.bfloat16), raw[:, :SEG]], 1)]
    for block in range(1, RAW // SEG):
        pieces.append(raw[:, block * SEG - TILE : (block + 1) * SEG])
    spans = jnp.concatenate(pieces, 0)
    out = sum(contract(spans, part, 1, 1) for part in split3(band)[::-1])
    return jnp.concatenate([out[b * rows : (b + 1) * rows] for b in range(RAW // SEG)], 1)


def whiten_rows(decimated, keep, table_ref):
    high, low = split2(decimated)
    table_high = table_ref[:SEG, :]
    spectrum = contract(low, table_high, 1, 0) + contract(high, table_ref[SEG:, :], 1, 0)
    spectrum = spectrum + contract(high, table_high, 1, 0)
    real_part, imag_part = spectrum[:, :NBIN], spectrum[:, NBIN:]
    power = real_part * real_part + imag_part * imag_part
    level = jnp.mean(power, -1, keepdims=True)
    scale = keep.astype(jnp.float32) * lax.rsqrt(0.5 * power + 0.5 * level + 1e-05)
    return jnp.concatenate([real_part * scale, imag_part * scale], 1).astype(jnp.bfloat16)


def arrange(piece_ref, spectra_ref):
    members, rows = piece_ref.shape[:2]
    width = rows // WINDOWS
    for pair in range(WINDOWS // 2):
        for quarter in range(4):
            block = piece_ref[:, pair * 2 * width : (pair + 1) * 2 * width, quarter * 128 : (quarter + 1) * 128]
            block = block.astype(jnp.float32)
            for half in range(2):
                turned = block[:, half * width : (half + 1) * width].reshape(members * width, 128).T
                start = (quarter % 2) * 128 * 32 + (quarter // 2) * WINDOWS + pair * 2 + half
                spectra_ref[pl.ds(start, 128, 32), :] = turned


def stack_kernel(same, per_step, entry_ref, rows_ref, *refs):
    if same:
        lag_ref, out_ref, cross_ref, row_spec = refs
    else:
        cols_ref, lag_ref, out_ref, cross_ref, row_spec, col_spec = refs

    @pl.when(pl.program_id(0) == 0)
    def _():
        arrange(rows_ref, row_spec)
        if not same:
            arrange(cols_ref, col_spec)

        def one_bin(f, carry):
            start = pl.multiple_of(f * 32, 32)
            left = row_spec[pl.ds(start, 32), :]
            right = left if same else col_spec[pl.ds(start, 32), :]
            turned = jnp.concatenate([right[WINDOWS:], -right[:WINDOWS]], 0)
            both = jnp.concatenate([right, turned], 1).astype(jnp.bfloat16)
            cross = contract(left.astype(jnp.bfloat16), both, 0, 0)
            cross_ref[pl.ds(f, TILE, STRIDE), :] = cross[:, :TILE]
            cross_ref[pl.ds(f + NBIN, TILE, STRIDE), :] = cross[:, TILE:]
            return carry

        lax.fori_loop(0, NBIN, one_bin, 0, unroll=8)

    base = pl.program_id(0) * per_step
    for group in range(per_step // 4):
        picked = []
        for member in range(4):
            start = pl.multiple_of((base + group * 4 + member) * STRIDE, 8)
            picked.append(cross_ref[pl.ds(start, 2 * NBIN), :].astype(jnp.bfloat16))
        stacked = contract(jnp.concatenate(picked, 1), lag_ref[...], 0, 0)
        out_ref[group * 4 : group * 4 + 4] = stacked.reshape(4, TILE, LAGS).astype(jnp.bfloat16)


def stack(gathered, table):
    members = TILE * WINDOWS // gathered.shape[1]
    same = gathered.shape[0] == members
    per_step = 8
    block = (members,) + gathered.shape[1:]
    spectra = pltpu.VMEM((2 * NBIN * WINDOWS, TILE), jnp.float32)
    if same:
        entry = table[0]
        sides = [pl.BlockSpec(block, lambda s, entry: (0, 0, 0))]
    else:
        entry = table[lax.axis_index("tiles")]
        sides = [
            pl.BlockSpec(block, lambda s, entry: (entry[0], 0, 0)),
            pl.BlockSpec(block, lambda s, entry: (entry[1], 0, 0)),
        ]
    return pl.pallas_call(
        functools.partial(stack_kernel, same, per_step),
        out_shape=jax.ShapeDtypeStruct((TILE, TILE, LAGS), jnp.bfloat16),
        grid_spec=pltpu.PrefetchScalarGridSpec(
            num_scalar_prefetch=1,
            grid=(TILE // per_step,),
            in_specs=sides + [pl.BlockSpec((2 * NBIN, LAGS), lambda s, entry: (0, 0))],
            out_specs=pl.BlockSpec((per_step, TILE, LAGS), lambda s, entry: (s, 0, 0)),
            scratch_shapes=[pltpu.VMEM((TILE * STRIDE, TILE), jnp.float32)] + [spectra] * len(sides),
        ),
        compiler_params=pltpu.CompilerParams(vmem_limit_bytes=60 << 20),
        cost_estimate=pl.CostEstimate(flops=10 << 30, bytes_accessed=12 << 20, transcendentals=0),
    )(entry, *[gathered] * len(sides), lag_table())


def other_core(me):
    return me + 1 - 2 * (me % 2)


def other_chip(me):
    return me + 2 - 4 * ((me // 2) % 2)


def remote(source, target, send, receive, peer):
    return pltpu.make_async_remote_copy(
        src_ref=source,
        dst_ref=target,
        send_sem=send,
        recv_sem=receive,
        device_id={"tiles": peer},
        device_id_type=pl.DeviceIdType.MESH,
    )


def front_kernel(
    devices, raw_ref, taps_ref, keep_ref, table_ref, out_ref,
    sum_buf, part_buf, common_buf, held,
    part_send, part_recv, common_send, common_recv,
    right_send, left_send, chip_send, core_send, held_recv, local_sem,
):
    me = lax.axis_index("tiles")
    channels = raw_ref.shape[1]
    rows = WINDOWS * channels
    barrier = pltpu.get_barrier_semaphore()
    all_owners = devices == WINDOWS

    def greet(k, carry):
        pl.semaphore_signal(
            barrier, inc=1, device_id={"tiles": (me + k) % devices}, device_id_type=pl.DeviceIdType.MESH
        )
        return carry

    lax.fori_loop(1, devices, greet, 0)
    filtered = filter_rows(raw_ref, taps_ref).reshape(WINDOWS, channels, SEG)
    sum_buf[...] = jnp.sum(filtered, 1, keepdims=True)
    pl.semaphore_wait(barrier, devices - 1)

    def part_copy(owner, slot):
        return remote(sum_buf.at[owner], part_buf.at[slot], part_send.at[owner], part_recv.at[slot], owner)

    def common_copy(owner, peer):
        return remote(common_buf.at[owner], common_buf.at[owner], common_send.at[peer], common_recv.at[owner], peer)

    def send_part(k, carry):
        owner = (me + k) % WINDOWS

        @pl.when(owner != me)
        def _():
            part_copy(owner, me).start()

        return carry

    lax.fori_loop(1 if all_owners else 0, WINDOWS, send_part, 0)

    @pl.when(me < WINDOWS)
    def _():
        part_buf[me] = sum_buf[me]

        def take(k, carry):
            part_copy(me, (me + k) % devices).wait_recv()
            return carry

        lax.fori_loop(1, devices, take, 0)
        common_buf[me] = jnp.sum(part_buf[...], 0)

        def give(k, carry):
            common_copy(me, (me + k) % devices).start()
            return carry

        lax.fori_loop(1, devices, give, 0)

    def take_common(k, carry):
        owner = (me + k) % WINDOWS

        @pl.when(owner != me)
        def _():
            common_copy(owner, me).wait_recv()

        return carry

    lax.fori_loop(1 if all_owners else 0, WINDOWS, take_common, 0)
    common = common_buf[...] / (channels * devices)
    decimated = (filtered - common).reshape(rows, SEG)
    keep = jnp.broadcast_to(keep_ref[...].astype(jnp.float32)[:, :, None], (WINDOWS, channels, NBIN))
    held[me] = whiten_rows(decimated, keep.reshape(rows, NBIN), table_ref)

    depth = devices // 4
    q, low = me // 4, me % 4
    chip, core = other_chip(me), other_core(me)

    def block_copy(block, send, peer):
        return remote(held.at[block], held.at[block], send, held_recv.at[block], peer)

    def to_right(level):
        return block_copy(4 * level + low, right_send.at[level], (me + 4) % devices)

    def to_left(level):
        return block_copy(4 * level + low, left_send.at[level], (me + devices - 4) % devices)

    def to_chip(level):
        return block_copy(4 * level + low, chip_send.at[level], chip)

    def to_core(block):
        return block_copy(block, core_send.at[block // 2], core)

    def arrived(block):
        block_copy(block, core_send.at[block // 2], core).wait_recv()
        keep_block(block)

    def keep_block(block):
        pltpu.make_async_copy(held.at[block], out_ref.at[block], local_sem.at[block]).start()

    def line_block(level, forward, go):
        block = 4 * level + low
        arrived(block)

        @pl.when(go)
        def _():
            forward(level).start()

        to_chip(level).start()
        to_core(block).start()

    def chip_block(level):
        block = 4 * level + other_chip(low)
        arrived(block)
        to_core(block).start()

    @pl.when(q < depth - 1)
    def _():
        to_right(q).start()

    @pl.when(q > 0)
    def _():
        to_left(q).start()

    to_chip(q).start()
    to_core(me).start()
    keep_block(me)

    def step(d, carry):
        @pl.when(q - d >= 0)
        def _():
            line_block(q - d, to_right, q < depth - 1)

        @pl.when(q + d < depth)
        def _():
            line_block(q + d, to_left, q > 0)

        @pl.when(d == 1)
        def _():
            chip_block(q)

        @pl.when((d > 1) & (q - d + 1 >= 0))
        def _():
            chip_block(q - d + 1)

        @pl.when((d > 1) & (q + d - 1 < depth))
        def _():
            chip_block(q + d - 1)

        return carry

    lax.fori_loop(1, depth + 1, step, 0)

    def from_core(pair, carry):
        arrived(2 * pair + core % 2)
        return carry

    lax.fori_loop(0, 2 * depth, from_core, 0)

    def finish(level, carry):
        @pl.when((level <= q) & (q < depth - 1))
        def _():
            to_right(level).wait_send()

        @pl.when((level >= q) & (q > 0))
        def _():
            to_left(level).wait_send()

        to_chip(level).wait_send()
        to_core(4 * level + low).wait_send()
        to_core(4 * level + other_chip(low)).wait_send()
        return carry

    lax.fori_loop(0, depth, finish, 0)

    def drain_part(k, carry):
        owner = (me + k) % WINDOWS

        @pl.when(owner != me)
        def _():
            part_copy(owner, me).wait_send()

        return carry

    lax.fori_loop(1 if all_owners else 0, WINDOWS, drain_part, 0)

    @pl.when(me < WINDOWS)
    def _():
        def drain(k, carry):
            common_copy(me, (me + k) % devices).wait_send()
            return carry

        lax.fori_loop(1, devices, drain, 0)

    def settle(block, carry):
        pltpu.make_async_copy(held.at[block], out_ref.at[block], local_sem.at[block]).wait()
        return carry

    lax.fori_loop(0, devices, settle, 0)


def front(devices, raw, fir, keep):
    rows = raw.shape[0] * raw.shape[1]
    depth = devices // 4
    dma = pltpu.SemaphoreType.DMA
    vmem = pl.BlockSpec(memory_space=pltpu.VMEM)
    line = pltpu.VMEM((WINDOWS, 1, SEG), jnp.float32)
    return pl.pallas_call(
        functools.partial(front_kernel, devices),
        out_shape=jax.ShapeDtypeStruct((devices, rows, 2 * NBIN), jnp.bfloat16),
        in_specs=[vmem] * 4,
        out_specs=pl.BlockSpec(memory_space=pl.ANY),
        scratch_shapes=[
            line, pltpu.VMEM((devices, 1, SEG), jnp.float32), line,
            pltpu.VMEM((devices, rows, 2 * NBIN), jnp.bfloat16),
            dma((WINDOWS,)), dma((devices,)), dma((devices,)), dma((WINDOWS,)),
            dma((depth,)), dma((depth,)), dma((depth,)), dma((2 * depth,)), dma((devices,)), dma((devices,)),
        ],
        compiler_params=pltpu.CompilerParams(
            collective_id=0, has_side_effects=True, vmem_limit_bytes=48 << 20
        ),
    )(raw, fir.reshape(1, TAPS), keep, dft_tables())


def local(raw, fir, keep, table):
    gathered = front(lax.axis_size("tiles"), raw, fir, keep)
    return stack(gathered, table)[None]


def solution(mesh):
    placed = (P(None, ("groups", "tiles"), None), P(), P(None, ("groups", "tiles")), P())
    return jax.shard_map(
        local,
        mesh=mesh,
        in_specs=placed,
        out_specs=P(("groups", "tiles"), None, None, None),
        check_vma=False,
    )
```

```python
import functools

import jax
import jax.numpy as jnp
import numpy as np
from jax import lax
from jax.experimental import pallas as pl
from jax.experimental.pallas import tpu as pltpu
from jax.sharding import PartitionSpec as P

WINDOWS = 16
TILE = 128
SEG = 512
LAGS = 256
TAPS = 64
DEC = 4
RAW = 2048
NBIN = 256
SPAN = 640
STRIDE = 520
PIECES = 2


def split2(x):
    high = x.astype(jnp.bfloat16)
    return high, (x - high.astype(jnp.float32)).astype(jnp.bfloat16)


def split3(x):
    high = x.astype(jnp.bfloat16)
    rest = x - high.astype(jnp.float32)
    middle = rest.astype(jnp.bfloat16)
    return high, middle, (rest - middle.astype(jnp.float32)).astype(jnp.bfloat16)


def contract(a, b, left, right):
    return lax.dot_general(a, b, (((left,), (right,)), ((), ())), preferred_element_type=jnp.float32)


def dft_tables():
    angle = 2.0 * np.pi / SEG * np.mod(np.arange(SEG)[:, None] * np.arange(NBIN)[None, :], SEG)
    table = np.concatenate([np.cos(angle), -np.sin(angle)], 1).astype(np.float32)
    high = table.astype(jnp.bfloat16)
    low = (table - high.astype(np.float32)).astype(jnp.bfloat16)
    return jnp.asarray(np.concatenate([high, low], 0))


def lag_table():
    freqs = np.arange(NBIN)
    shifts = np.arange(LAGS) - LAGS // 2
    angle = 2.0 * np.pi / SEG * np.mod(freqs[:, None] * shifts[None, :], SEG)
    weight = np.where(freqs == 0, 1.0, 2.0)[:, None] / np.sqrt(WINDOWS * NBIN)
    table = np.concatenate([weight * np.cos(angle), -weight * np.sin(angle)], 0)
    return jnp.asarray(table.astype(np.float32).astype(jnp.bfloat16))


def filter_rows(raw_ref, taps_ref):
    rows = raw_ref.shape[0] * raw_ref.shape[1]
    raw = raw_ref[...].astype(jnp.float32).reshape(rows, RAW).astype(jnp.bfloat16)
    taps = jnp.broadcast_to(taps_ref[...], (8, TAPS))
    places = lax.broadcasted_iota(jnp.int32, (TAPS, SPAN), 0) + lax.broadcasted_iota(jnp.int32, (TAPS, SPAN), 1)
    pick = jnp.where(places == TILE, 1.0, 0.0).astype(jnp.bfloat16)
    spread = sum(contract(part, pick, 1, 0) for part in split3(taps)[::-1])
    band = jnp.broadcast_to(spread[:1], (TILE, SPAN))
    index = lax.broadcasted_iota(jnp.int32, (TILE, SPAN), 0)
    for bit in range(7):
        band = jnp.where((index >> bit) & 1 == 1, pltpu.roll(band, DEC << bit, 1), band)
    pieces = [jnp.concatenate([jnp.zeros((rows, TILE), jnp.bfloat16), raw[:, :SEG]], 1)]
    for block in range(1, RAW // SEG):
        pieces.append(raw[:, block * SEG - TILE : (block + 1) * SEG])
    spans = jnp.concatenate(pieces, 0)
    out = sum(contract(spans, part, 1, 1) for part in split3(band)[::-1])
    return jnp.concatenate([out[b * rows : (b + 1) * rows] for b in range(RAW // SEG)], 1)


def whiten_rows(decimated, keep, table_ref):
    high, low = split2(decimated)
    table_high = table_ref[:SEG, :]
    spectrum = contract(low, table_high, 1, 0) + contract(high, table_ref[SEG:, :], 1, 0)
    spectrum = spectrum + contract(high, table_high, 1, 0)
    real_part, imag_part = spectrum[:, :NBIN], spectrum[:, NBIN:]
    power = real_part * real_part + imag_part * imag_part
    level = jnp.mean(power, -1, keepdims=True)
    scale = keep.astype(jnp.float32) * lax.rsqrt(0.5 * power + 0.5 * level + 1e-05)
    return jnp.concatenate([real_part * scale, imag_part * scale], 1).astype(jnp.bfloat16)


def arrange(piece_ref, spectra_ref):
    members, rows = piece_ref.shape[:2]
    width = rows // WINDOWS
    for pair in range(WINDOWS // 2):
        for quarter in range(4):
            block = piece_ref[:, pair * 2 * width : (pair + 1) * 2 * width, quarter * 128 : (quarter + 1) * 128]
            block = block.astype(jnp.float32)
            for half in range(2):
                turned = block[:, half * width : (half + 1) * width].reshape(members * width, 128).T
                start = (quarter % 2) * 128 * 32 + (quarter // 2) * WINDOWS + pair * 2 + half
                spectra_ref[pl.ds(start, 128, 32), :] = turned


def stack_kernel(same, per_step, entry_ref, rows_ref, *refs):
    if same:
        lag_ref, out_ref, cross_ref, row_spec = refs
    else:
        cols_ref, lag_ref, out_ref, cross_ref, row_spec, col_spec = refs

    @pl.when(pl.program_id(0) == 0)
    def _():
        arrange(rows_ref, row_spec)
        if not same:
            arrange(cols_ref, col_spec)

        def one_bin(f, carry):
            start = pl.multiple_of(f * 32, 32)
            left = row_spec[pl.ds(start, 32), :]
            right = left if same else col_spec[pl.ds(start, 32), :]
            turned = jnp.concatenate([right[WINDOWS:], -right[:WINDOWS]], 0)
            both = jnp.concatenate([right, turned], 1).astype(jnp.bfloat16)
            cross = contract(left.astype(jnp.bfloat16), both, 0, 0)
            cross_ref[pl.ds(f, TILE, STRIDE), :] = cross[:, :TILE]
            cross_ref[pl.ds(f + NBIN, TILE, STRIDE), :] = cross[:, TILE:]
            return carry

        lax.fori_loop(0, NBIN, one_bin, 0, unroll=64)

    base = pl.program_id(0) * per_step
    for group in range(per_step // 4):
        picked = []
        for member in range(4):
            start = pl.multiple_of((base + group * 4 + member) * STRIDE, 8)
            picked.append(cross_ref[pl.ds(start, 2 * NBIN), :].astype(jnp.bfloat16))
        stacked = contract(jnp.concatenate(picked, 1), lag_ref[...], 0, 0)
        out_ref[group * 4 : group * 4 + 4] = stacked.reshape(4, TILE, LAGS).astype(jnp.bfloat16)


def stack(gathered, table):
    members = TILE * WINDOWS // gathered.shape[1]
    same = gathered.shape[0] == members
    per_step = 32
    block = (members,) + gathered.shape[1:]
    spectra = pltpu.VMEM((2 * NBIN * WINDOWS, TILE), jnp.float32)
    if same:
        entry = table
        sides = [pl.BlockSpec(block, lambda s, entry: (0, 0, 0))]
    else:
        entry = table[lax.axis_index("tiles")]
        sides = [
            pl.BlockSpec(block, lambda s, entry: (entry[0], 0, 0)),
            pl.BlockSpec(block, lambda s, entry: (entry[1], 0, 0)),
        ]
    return pl.pallas_call(
        functools.partial(stack_kernel, same, per_step),
        out_shape=jax.ShapeDtypeStruct((TILE, TILE, LAGS), jnp.bfloat16),
        grid_spec=pltpu.PrefetchScalarGridSpec(
            num_scalar_prefetch=1,
            grid=(TILE // per_step,),
            in_specs=sides + [pl.BlockSpec((2 * NBIN, LAGS), lambda s, entry: (0, 0))],
            out_specs=pl.BlockSpec((per_step, TILE, LAGS), lambda s, entry: (s, 0, 0)),
            scratch_shapes=[pltpu.VMEM((TILE * STRIDE, TILE), jnp.float32)] + [spectra] * len(sides),
        ),
        compiler_params=pltpu.CompilerParams(vmem_limit_bytes=60 << 20),
        cost_estimate=pl.CostEstimate(flops=10 << 30, bytes_accessed=12 << 20, transcendentals=0),
    )(entry, *[gathered] * len(sides), lag_table())


def other_core(me):
    return me + 1 - 2 * (me % 2)


def other_chip(me):
    return me + 2 - 4 * ((me // 2) % 2)


def remote(source, target, send, receive, peer):
    return pltpu.make_async_remote_copy(
        src_ref=source,
        dst_ref=target,
        send_sem=send,
        recv_sem=receive,
        device_id={"tiles": peer},
        device_id_type=pl.DeviceIdType.MESH,
    )


def front_kernel(
    devices, raw_hbm, taps_ref, keep_ref, table_hbm, out_ref,
    raw_ref, table_ref, load_sem, sum_buf, part_buf, common_buf, held,
    part_send, part_recv, common_send, common_recv,
    right_send, left_send, chip_send, core_send, held_recv, local_sem,
):
    me = lax.axis_index("tiles")
    channels = raw_ref.shape[1]
    rows = WINDOWS * channels
    barrier = pltpu.get_barrier_semaphore()
    all_owners = devices == WINDOWS

    def greet(k, carry):
        pl.semaphore_signal(
            barrier, inc=1, device_id={"tiles": (me + k) % devices}, device_id_type=pl.DeviceIdType.MESH
        )
        return carry

    load_raw = pltpu.make_async_copy(raw_hbm, raw_ref, load_sem.at[0])
    load_raw.start()
    load_table = pltpu.make_async_copy(table_hbm, table_ref, load_sem.at[1])
    load_table.start()
    lax.fori_loop(1, devices, greet, 0)
    load_raw.wait()
    filtered = filter_rows(raw_ref, taps_ref).reshape(WINDOWS, channels, SEG)
    sum_buf[...] = jnp.sum(filtered, 1, keepdims=True)
    pl.semaphore_wait(barrier, devices - 1)

    def part_copy(owner, slot):
        return remote(sum_buf.at[owner], part_buf.at[slot], part_send.at[owner], part_recv.at[slot], owner)

    def common_copy(owner, peer):
        return remote(common_buf.at[owner], common_buf.at[owner], common_send.at[peer], common_recv.at[owner], peer)

    def send_part(k, carry):
        owner = (me + k) % WINDOWS

        @pl.when(owner != me)
        def _():
            part_copy(owner, me).start()

        return carry

    lax.fori_loop(1 if all_owners else 0, WINDOWS, send_part, 0)

    @pl.when(me < WINDOWS)
    def _():
        part_buf[me] = sum_buf[me]

        def take(k, carry):
            part_copy(me, (me + k) % devices).wait_recv()
            return carry

        lax.fori_loop(1, devices, take, 0)
        common_buf[me] = jnp.sum(part_buf[...], 0)

        def give(k, carry):
            common_copy(me, (me + k) % devices).start()
            return carry

        lax.fori_loop(1, devices, give, 0)

    def take_common(k, carry):
        owner = (me + k) % WINDOWS

        @pl.when(owner != me)
        def _():
            common_copy(owner, me).wait_recv()

        return carry

    lax.fori_loop(1 if all_owners else 0, WINDOWS, take_common, 0)
    common = common_buf[...] / (channels * devices)
    decimated = (filtered - common).reshape(rows, SEG)
    keep = jnp.broadcast_to(keep_ref[...].astype(jnp.float32)[:, :, None], (WINDOWS, channels, NBIN))
    load_table.wait()
    whitened = whiten_rows(decimated, keep.reshape(rows, NBIN), table_ref)
    held[me] = whitened.reshape(PIECES, rows // PIECES, 2 * NBIN)

    depth = devices // 4
    q, low = me // 4, me % 4
    chip, core = other_chip(me), other_core(me)

    def block_copy(block, piece, send, peer):
        return remote(held.at[block, piece], held.at[block, piece], send, held_recv.at[block, piece], peer)

    def to_right(level, piece):
        return block_copy(4 * level + low, piece, right_send.at[level, piece], (me + 4) % devices)

    def to_left(level, piece):
        return block_copy(4 * level + low, piece, left_send.at[level, piece], (me + devices - 4) % devices)

    def to_chip(level, piece):
        return block_copy(4 * level + low, piece, chip_send.at[level, piece], chip)

    def to_core(block, piece):
        return block_copy(block, piece, core_send.at[block // 2, piece], core)

    def local_copy(block, piece):
        part = rows // PIECES
        return pltpu.make_async_copy(
            held.at[block, piece], out_ref.at[block, pl.ds(piece * part, part)], local_sem.at[block, piece]
        )

    def arrived(block, piece):
        to_core(block, piece).wait_recv()
        local_copy(block, piece).start()

    def line_block(level, piece, forward, go):
        block = 4 * level + low
        arrived(block, piece)

        @pl.when(go)
        def _():
            forward(level, piece).start()

        to_chip(level, piece).start()
        to_core(block, piece).start()

    def chip_block(level, piece):
        block = 4 * level + other_chip(low)
        arrived(block, piece)
        to_core(block, piece).start()

    for piece in range(PIECES):
        @pl.when(q < depth - 1)
        def _():
            to_right(q, piece).start()

        @pl.when(q > 0)
        def _():
            to_left(q, piece).start()

        to_chip(q, piece).start()

    for piece in range(PIECES):
        to_core(me, piece).start()
        local_copy(me, piece).start()

    def step(d, carry):
        for piece in range(PIECES):
            @pl.when(q - d >= 0)
            def _():
                line_block(q - d, piece, to_right, q < depth - 1)

            @pl.when(q + d < depth)
            def _():
                line_block(q + d, piece, to_left, q > 0)

        for piece in range(PIECES):
            @pl.when(d == 1)
            def _():
                chip_block(q, piece)

            @pl.when((d > 1) & (q - d + 1 >= 0))
            def _():
                chip_block(q - d + 1, piece)

            @pl.when((d > 1) & (q + d - 1 < depth))
            def _():
                chip_block(q + d - 1, piece)

        return carry

    lax.fori_loop(1, depth + 1, step, 0)

    def from_core(pair, carry):
        for piece in range(PIECES):
            arrived(2 * pair + core % 2, piece)
        return carry

    lax.fori_loop(0, 2 * depth, from_core, 0)

    def finish(level, carry):
        for piece in range(PIECES):
            @pl.when((level <= q) & (q < depth - 1))
            def _():
                to_right(level, piece).wait_send()

            @pl.when((level >= q) & (q > 0))
            def _():
                to_left(level, piece).wait_send()

            to_chip(level, piece).wait_send()
            to_core(4 * level + low, piece).wait_send()
            to_core(4 * level + other_chip(low), piece).wait_send()
        return carry

    lax.fori_loop(0, depth, finish, 0)

    def drain_part(k, carry):
        owner = (me + k) % WINDOWS

        @pl.when(owner != me)
        def _():
            part_copy(owner, me).wait_send()

        return carry

    lax.fori_loop(1 if all_owners else 0, WINDOWS, drain_part, 0)

    @pl.when(me < WINDOWS)
    def _():
        def drain(k, carry):
            common_copy(me, (me + k) % devices).wait_send()
            return carry

        lax.fori_loop(1, devices, drain, 0)

    def settle(block, carry):
        for piece in range(PIECES):
            local_copy(block, piece).wait()
        return carry

    lax.fori_loop(0, devices, settle, 0)


def front(devices, raw, fir, keep):
    rows = raw.shape[0] * raw.shape[1]
    depth = devices // 4
    dma = pltpu.SemaphoreType.DMA
    vmem = pl.BlockSpec(memory_space=pltpu.VMEM)
    hbm = pl.BlockSpec(memory_space=pl.ANY)
    line = pltpu.VMEM((WINDOWS, 1, SEG), jnp.float32)
    return pl.pallas_call(
        functools.partial(front_kernel, devices),
        out_shape=jax.ShapeDtypeStruct((devices, rows, 2 * NBIN), jnp.bfloat16),
        in_specs=[hbm, vmem, vmem, hbm],
        out_specs=pl.BlockSpec(memory_space=pl.ANY),
        scratch_shapes=[
            pltpu.VMEM(raw.shape, jnp.bfloat16), pltpu.VMEM((2 * SEG, 2 * NBIN), jnp.bfloat16), dma((2,)),
            line, pltpu.VMEM((devices, 1, SEG), jnp.float32), line,
            pltpu.VMEM((devices, PIECES, rows // PIECES, 2 * NBIN), jnp.bfloat16),
            dma((WINDOWS,)), dma((devices,)), dma((devices,)), dma((WINDOWS,)),
            dma((depth, PIECES)), dma((depth, PIECES)), dma((depth, PIECES)), dma((2 * depth, PIECES)),
            dma((devices, PIECES)), dma((devices, PIECES)),
        ],
        compiler_params=pltpu.CompilerParams(
            collective_id=0, has_side_effects=True, vmem_limit_bytes=60 << 20
        ),
    )(raw, fir.reshape(1, TAPS), keep, dft_tables())


def local(raw, fir, keep, table):
    gathered = front(lax.axis_size("tiles"), raw, fir, keep)
    return stack(gathered, table)[None]


def solution(mesh):
    placed = (P(None, ("groups", "tiles"), None), P(), P(None, ("groups", "tiles")), P())
    return jax.shard_map(
        local,
        mesh=mesh,
        in_specs=placed,
        out_specs=P(("groups", "tiles"), None, None, None),
        check_vma=False,
    )
```

```python
import functools

import jax
import jax.numpy as jnp
import numpy as np
from jax import lax
from jax.experimental import pallas as pl
from jax.experimental.pallas import tpu as pltpu
from jax.sharding import PartitionSpec as P

WINDOWS = 16
TILE = 128
SEG = 512
LAGS = 256
TAPS = 64
DEC = 4
RAW = 2048
NBIN = 256
SPAN = 640
STRIDE = 520
PIECES = 2


def split2(x):
    high = x.astype(jnp.bfloat16)
    return high, (x - high.astype(jnp.float32)).astype(jnp.bfloat16)


def split3(x):
    high = x.astype(jnp.bfloat16)
    rest = x - high.astype(jnp.float32)
    middle = rest.astype(jnp.bfloat16)
    return high, middle, (rest - middle.astype(jnp.float32)).astype(jnp.bfloat16)


def contract(a, b, left, right):
    return lax.dot_general(a, b, (((left,), (right,)), ((), ())), preferred_element_type=jnp.float32)


def dft_tables():
    angle = 2.0 * np.pi / SEG * np.mod(np.arange(SEG)[:, None] * np.arange(NBIN)[None, :], SEG)
    table = np.concatenate([np.cos(angle), -np.sin(angle)], 1).astype(np.float32)
    high = table.astype(jnp.bfloat16)
    low = (table - high.astype(np.float32)).astype(jnp.bfloat16)
    return jnp.asarray(np.concatenate([high, low], 0))


def lag_table():
    freqs = np.arange(NBIN)
    shifts = np.arange(LAGS) - LAGS // 2
    angle = 2.0 * np.pi / SEG * np.mod(freqs[:, None] * shifts[None, :], SEG)
    weight = np.where(freqs == 0, 1.0, 2.0)[:, None] / np.sqrt(WINDOWS * NBIN)
    table = np.concatenate([weight * np.cos(angle), -weight * np.sin(angle)], 0)
    return jnp.asarray(table.astype(np.float32).astype(jnp.bfloat16))


def filter_rows(raw_ref, taps_ref):
    rows = raw_ref.shape[0] * raw_ref.shape[1]
    raw = raw_ref[...].astype(jnp.float32).reshape(rows, RAW).astype(jnp.bfloat16)
    taps = jnp.broadcast_to(taps_ref[...], (8, TAPS))
    places = lax.broadcasted_iota(jnp.int32, (TAPS, SPAN), 0) + lax.broadcasted_iota(jnp.int32, (TAPS, SPAN), 1)
    pick = jnp.where(places == TILE, 1.0, 0.0).astype(jnp.bfloat16)
    spread = sum(contract(part, pick, 1, 0) for part in split3(taps)[::-1])
    band = jnp.broadcast_to(spread[:1], (TILE, SPAN))
    index = lax.broadcasted_iota(jnp.int32, (TILE, SPAN), 0)
    for bit in range(7):
        band = jnp.where((index >> bit) & 1 == 1, pltpu.roll(band, DEC << bit, 1), band)
    pieces = [jnp.concatenate([jnp.zeros((rows, TILE), jnp.bfloat16), raw[:, :SEG]], 1)]
    for block in range(1, RAW // SEG):
        pieces.append(raw[:, block * SEG - TILE : (block + 1) * SEG])
    spans = jnp.concatenate(pieces, 0)
    out = sum(contract(spans, part, 1, 1) for part in split3(band)[::-1])
    return jnp.concatenate([out[b * rows : (b + 1) * rows] for b in range(RAW // SEG)], 1)


def whiten_rows(decimated, keep, table_ref):
    high, low = split2(decimated)
    table_high = table_ref[:SEG, :]
    spectrum = contract(low, table_high, 1, 0) + contract(high, table_ref[SEG:, :], 1, 0)
    spectrum = spectrum + contract(high, table_high, 1, 0)
    real_part, imag_part = spectrum[:, :NBIN], spectrum[:, NBIN:]
    power = real_part * real_part + imag_part * imag_part
    level = jnp.mean(power, -1, keepdims=True)
    scale = keep.astype(jnp.float32) * lax.rsqrt(0.5 * power + 0.5 * level + 1e-05)
    return jnp.concatenate([real_part * scale, imag_part * scale], 1).astype(jnp.bfloat16)


def arrange(piece_ref, spectra_ref):
    members, rows = piece_ref.shape[:2]
    width = rows // WINDOWS
    for pair in range(WINDOWS // 2):
        for quarter in range(4):
            block = piece_ref[:, pair * 2 * width : (pair + 1) * 2 * width, quarter * 128 : (quarter + 1) * 128]
            block = block.astype(jnp.float32)
            for half in range(2):
                turned = block[:, half * width : (half + 1) * width].reshape(members * width, 128).T
                start = (quarter % 2) * 128 * 32 + (quarter // 2) * WINDOWS + pair * 2 + half
                spectra_ref[pl.ds(start, 128, 32), :] = turned


def stack_kernel(same, per_step, *refs):
    if same:
        rows_ref, lag_ref, out_ref, cross_ref, row_spec = refs
    else:
        _, rows_ref, cols_ref, lag_ref, out_ref, cross_ref, row_spec, col_spec = refs

    @pl.when(pl.program_id(0) == 0)
    def _():
        arrange(rows_ref, row_spec)
        if not same:
            arrange(cols_ref, col_spec)

        def one_bin(f, carry):
            start = pl.multiple_of(f * 32, 32)
            left = row_spec[pl.ds(start, 32), :]
            right = left if same else col_spec[pl.ds(start, 32), :]
            turned = jnp.concatenate([right[WINDOWS:], -right[:WINDOWS]], 0)
            both = jnp.concatenate([right, turned], 1).astype(jnp.bfloat16)
            cross = contract(left.astype(jnp.bfloat16), both, 0, 0)
            cross_ref[pl.ds(f, TILE, STRIDE), :] = cross[:, :TILE]
            cross_ref[pl.ds(f + NBIN, TILE, STRIDE), :] = cross[:, TILE:]
            return carry

        lax.fori_loop(0, NBIN, one_bin, 0, unroll=64)

    base = pl.program_id(0) * per_step
    for group in range(per_step // 4):
        picked = []
        for member in range(4):
            start = pl.multiple_of((base + group * 4 + member) * STRIDE, 8)
            picked.append(cross_ref[pl.ds(start, 2 * NBIN), :].astype(jnp.bfloat16))
        stacked = contract(jnp.concatenate(picked, 1), lag_ref[...], 0, 0)
        out_ref[group * 4 : group * 4 + 4] = stacked.reshape(4, TILE, LAGS).astype(jnp.bfloat16)


def stack(gathered, table):
    members = TILE * WINDOWS // gathered.shape[1]
    same = gathered.shape[0] == members
    per_step = 32
    block = (members,) + gathered.shape[1:]
    spectra = pltpu.VMEM((2 * NBIN * WINDOWS, TILE), jnp.float32)
    if same:
        prefetch = []
        sides = [pl.BlockSpec(block, lambda s: (0, 0, 0))]
    else:
        prefetch = [table[lax.axis_index("tiles")]]
        sides = [
            pl.BlockSpec(block, lambda s, entry: (entry[0], 0, 0)),
            pl.BlockSpec(block, lambda s, entry: (entry[1], 0, 0)),
        ]
    return pl.pallas_call(
        functools.partial(stack_kernel, same, per_step),
        out_shape=jax.ShapeDtypeStruct((TILE, TILE, LAGS), jnp.bfloat16),
        grid_spec=pltpu.PrefetchScalarGridSpec(
            num_scalar_prefetch=len(prefetch),
            grid=(TILE // per_step,),
            in_specs=sides + [pl.BlockSpec((2 * NBIN, LAGS), lambda s, *entry: (0, 0))],
            out_specs=pl.BlockSpec((per_step, TILE, LAGS), lambda s, *entry: (s, 0, 0)),
            scratch_shapes=[pltpu.VMEM((TILE * STRIDE, TILE), jnp.float32)] + [spectra] * len(sides),
        ),
        compiler_params=pltpu.CompilerParams(vmem_limit_bytes=60 << 20),
        cost_estimate=pl.CostEstimate(flops=10 << 30, bytes_accessed=12 << 20, transcendentals=0),
    )(*prefetch, *[gathered] * len(sides), lag_table())


def other_core(me):
    return me + 1 - 2 * (me % 2)


def other_chip(me):
    return me + 2 - 4 * ((me // 2) % 2)


def remote(source, target, send, receive, peer):
    return pltpu.make_async_remote_copy(
        src_ref=source,
        dst_ref=target,
        send_sem=send,
        recv_sem=receive,
        device_id={"tiles": peer},
        device_id_type=pl.DeviceIdType.MESH,
    )


def front_kernel(
    devices, raw_hbm, taps_ref, keep_ref, table_hbm, out_ref,
    raw_ref, table_ref, load_sem, sum_buf, part_buf, common_buf, held,
    part_send, part_recv, common_send, common_recv,
    right_send, left_send, chip_send, core_send, held_recv, local_sem,
):
    me = lax.axis_index("tiles")
    channels = raw_ref.shape[1]
    rows = WINDOWS * channels
    barrier = pltpu.get_barrier_semaphore()
    all_owners = devices == WINDOWS

    def greet(k, carry):
        pl.semaphore_signal(
            barrier, inc=1, device_id={"tiles": (me + k) % devices}, device_id_type=pl.DeviceIdType.MESH
        )
        return carry

    load_raw = pltpu.make_async_copy(raw_hbm, raw_ref, load_sem.at[0])
    load_raw.start()
    load_table = pltpu.make_async_copy(table_hbm, table_ref, load_sem.at[1])
    load_table.start()
    lax.fori_loop(1, devices, greet, 0)
    load_raw.wait()
    filtered = filter_rows(raw_ref, taps_ref).reshape(WINDOWS, channels, SEG)
    sum_buf[...] = jnp.sum(filtered, 1, keepdims=True)
    pl.semaphore_wait(barrier, devices - 1)

    def part_copy(owner, slot):
        return remote(sum_buf.at[owner], part_buf.at[slot], part_send.at[owner], part_recv.at[slot], owner)

    def common_copy(owner, peer):
        return remote(common_buf.at[owner], common_buf.at[owner], common_send.at[peer], common_recv.at[owner], peer)

    def send_part(k, carry):
        owner = (me + k) % WINDOWS

        @pl.when(owner != me)
        def _():
            part_copy(owner, me).start()

        return carry

    lax.fori_loop(1 if all_owners else 0, WINDOWS, send_part, 0)

    @pl.when(me < WINDOWS)
    def _():
        part_buf[me] = sum_buf[me]

        def take(k, carry):
            part_copy(me, (me + k) % devices).wait_recv()
            return carry

        lax.fori_loop(1, devices, take, 0)
        common_buf[me] = jnp.sum(part_buf[...], 0)

        def give(k, carry):
            common_copy(me, (me + k) % devices).start()
            return carry

        lax.fori_loop(1, devices, give, 0)

    def take_common(k, carry):
        owner = (me + k) % WINDOWS

        @pl.when(owner != me)
        def _():
            common_copy(owner, me).wait_recv()

        return carry

    lax.fori_loop(1 if all_owners else 0, WINDOWS, take_common, 0)
    common = common_buf[...] / (channels * devices)
    decimated = (filtered - common).reshape(rows, SEG)
    keep = jnp.broadcast_to(keep_ref[...].astype(jnp.float32).T[:, :, None], (WINDOWS, channels, NBIN))
    load_table.wait()
    whitened = whiten_rows(decimated, keep.reshape(rows, NBIN), table_ref)
    held[me] = whitened.reshape(PIECES, rows // PIECES, 2 * NBIN)

    depth = devices // 4
    q, low = me // 4, me % 4
    chip, core = other_chip(me), other_core(me)

    def block_copy(block, piece, send, peer):
        return remote(held.at[block, piece], held.at[block, piece], send, held_recv.at[block, piece], peer)

    def to_right(level, piece):
        return block_copy(4 * level + low, piece, right_send.at[level, piece], (me + 4) % devices)

    def to_left(level, piece):
        return block_copy(4 * level + low, piece, left_send.at[level, piece], (me + devices - 4) % devices)

    def to_chip(level, piece):
        return block_copy(4 * level + low, piece, chip_send.at[level, piece], chip)

    def to_core(block, piece):
        return block_copy(block, piece, core_send.at[block // 2, piece], core)

    def local_copy(block, piece):
        part = rows // PIECES
        return pltpu.make_async_copy(
            held.at[block, piece], out_ref.at[block, pl.ds(piece * part, part)], local_sem.at[block, piece]
        )

    def arrived(block, piece):
        to_core(block, piece).wait_recv()
        local_copy(block, piece).start()

    def line_block(level, piece, forward, go):
        block = 4 * level + low
        arrived(block, piece)

        @pl.when(go)
        def _():
            forward(level, piece).start()

        to_chip(level, piece).start()
        to_core(block, piece).start()

    def chip_block(level, piece):
        block = 4 * level + other_chip(low)
        arrived(block, piece)
        to_core(block, piece).start()

    for piece in range(PIECES):
        @pl.when(q < depth - 1)
        def _():
            to_right(q, piece).start()

        @pl.when(q > 0)
        def _():
            to_left(q, piece).start()

        to_chip(q, piece).start()

    for piece in range(PIECES):
        to_core(me, piece).start()
        local_copy(me, piece).start()

    def step(d, carry):
        for piece in range(PIECES):
            @pl.when(q - d >= 0)
            def _():
                line_block(q - d, piece, to_right, q < depth - 1)

            @pl.when(q + d < depth)
            def _():
                line_block(q + d, piece, to_left, q > 0)

        for piece in range(PIECES):
            @pl.when(d == 1)
            def _():
                chip_block(q, piece)

            @pl.when((d > 1) & (q - d + 1 >= 0))
            def _():
                chip_block(q - d + 1, piece)

            @pl.when((d > 1) & (q + d - 1 < depth))
            def _():
                chip_block(q + d - 1, piece)

        return carry

    lax.fori_loop(1, depth + 1, step, 0)

    def from_core(pair, carry):
        for piece in range(PIECES):
            arrived(2 * pair + core % 2, piece)
        return carry

    lax.fori_loop(0, 2 * depth, from_core, 0)

    def finish(level, carry):
        for piece in range(PIECES):
            @pl.when((level <= q) & (q < depth - 1))
            def _():
                to_right(level, piece).wait_send()

            @pl.when((level >= q) & (q > 0))
            def _():
                to_left(level, piece).wait_send()

            to_chip(level, piece).wait_send()
            to_core(4 * level + low, piece).wait_send()
            to_core(4 * level + other_chip(low), piece).wait_send()
        return carry

    lax.fori_loop(0, depth, finish, 0)

    def drain_part(k, carry):
        owner = (me + k) % WINDOWS

        @pl.when(owner != me)
        def _():
            part_copy(owner, me).wait_send()

        return carry

    lax.fori_loop(1 if all_owners else 0, WINDOWS, drain_part, 0)

    @pl.when(me < WINDOWS)
    def _():
        def drain(k, carry):
            common_copy(me, (me + k) % devices).wait_send()
            return carry

        lax.fori_loop(1, devices, drain, 0)

    def settle(block, carry):
        for piece in range(PIECES):
            local_copy(block, piece).wait()
        return carry

    lax.fori_loop(0, devices, settle, 0)


def front(devices, raw, fir, keep):
    rows = raw.shape[0] * raw.shape[1]
    depth = devices // 4
    dma = pltpu.SemaphoreType.DMA
    vmem = pl.BlockSpec(memory_space=pltpu.VMEM)
    hbm = pl.BlockSpec(memory_space=pl.ANY)
    line = pltpu.VMEM((WINDOWS, 1, SEG), jnp.float32)
    return pl.pallas_call(
        functools.partial(front_kernel, devices),
        out_shape=jax.ShapeDtypeStruct((devices, rows, 2 * NBIN), jnp.bfloat16),
        in_specs=[hbm, vmem, vmem, hbm],
        out_specs=pl.BlockSpec(memory_space=pl.ANY),
        scratch_shapes=[
            pltpu.VMEM(raw.shape, jnp.bfloat16), pltpu.VMEM((2 * SEG, 2 * NBIN), jnp.bfloat16), dma((2,)),
            line, pltpu.VMEM((devices, 1, SEG), jnp.float32), line,
            pltpu.VMEM((devices, PIECES, rows // PIECES, 2 * NBIN), jnp.bfloat16),
            dma((WINDOWS,)), dma((devices,)), dma((devices,)), dma((WINDOWS,)),
            dma((depth, PIECES)), dma((depth, PIECES)), dma((depth, PIECES)), dma((2 * depth, PIECES)),
            dma((devices, PIECES)), dma((devices, PIECES)),
        ],
        compiler_params=pltpu.CompilerParams(
            collective_id=0, has_side_effects=True, vmem_limit_bytes=60 << 20
        ),
    )(raw, fir.reshape(1, TAPS), keep.T, dft_tables())


def local(raw, fir, keep, table):
    gathered = front(lax.axis_size("tiles"), raw, fir, keep)
    return stack(gathered, table)[None]


def solution(mesh):
    placed = (P(None, ("groups", "tiles"), None), P(), P(None, ("groups", "tiles")), P())
    return jax.shard_map(
        local,
        mesh=mesh,
        in_specs=placed,
        out_specs=P(("groups", "tiles"), None, None, None),
        check_vma=False,
    )
```

```python
import functools

import jax
import jax.numpy as jnp
import numpy as np
from jax import lax
from jax.experimental import pallas as pl
from jax.experimental.pallas import tpu as pltpu
from jax.sharding import PartitionSpec as P

WINDOWS = 16
TILE = 128
SEG = 512
LAGS = 256
TAPS = 64
DEC = 4
RAW = 2048
NBIN = 256
SPAN = 640
STRIDE = 520
PIECES = 4


def split2(x):
    high = x.astype(jnp.bfloat16)
    return high, (x - high.astype(jnp.float32)).astype(jnp.bfloat16)


def split3(x):
    high = x.astype(jnp.bfloat16)
    rest = x - high.astype(jnp.float32)
    middle = rest.astype(jnp.bfloat16)
    return high, middle, (rest - middle.astype(jnp.float32)).astype(jnp.bfloat16)


def contract(a, b, left, right):
    return lax.dot_general(a, b, (((left,), (right,)), ((), ())), preferred_element_type=jnp.float32)


def dft_tables():
    angle = 2.0 * np.pi / SEG * np.mod(np.arange(SEG)[:, None] * np.arange(NBIN)[None, :], SEG)
    table = np.concatenate([np.cos(angle), -np.sin(angle)], 1).astype(np.float32)
    high = table.astype(jnp.bfloat16)
    low = (table - high.astype(np.float32)).astype(jnp.bfloat16)
    return jnp.asarray(np.concatenate([high, low], 0))


def lag_table():
    freqs = np.arange(NBIN)
    shifts = np.arange(LAGS) - LAGS // 2
    angle = 2.0 * np.pi / SEG * np.mod(freqs[:, None] * shifts[None, :], SEG)
    weight = np.where(freqs == 0, 1.0, 2.0)[:, None] / np.sqrt(WINDOWS * NBIN)
    table = np.concatenate([weight * np.cos(angle), -weight * np.sin(angle)], 0)
    return jnp.asarray(table.astype(np.float32).astype(jnp.bfloat16))


def filter_rows(raw_ref, taps_ref):
    rows = raw_ref.shape[0] * raw_ref.shape[1]
    raw = raw_ref[...].astype(jnp.float32).reshape(rows, RAW).astype(jnp.bfloat16)
    taps = jnp.broadcast_to(taps_ref[...], (8, TAPS))
    places = lax.broadcasted_iota(jnp.int32, (TAPS, SPAN), 0) + lax.broadcasted_iota(jnp.int32, (TAPS, SPAN), 1)
    pick = jnp.where(places == TILE, 1.0, 0.0).astype(jnp.bfloat16)
    spread = sum(contract(part, pick, 1, 0) for part in split3(taps)[::-1])
    band = jnp.broadcast_to(spread[:1], (TILE, SPAN))
    index = lax.broadcasted_iota(jnp.int32, (TILE, SPAN), 0)
    for bit in range(7):
        band = jnp.where((index >> bit) & 1 == 1, pltpu.roll(band, DEC << bit, 1), band)
    pieces = [jnp.concatenate([jnp.zeros((rows, TILE), jnp.bfloat16), raw[:, :SEG]], 1)]
    for block in range(1, RAW // SEG):
        pieces.append(raw[:, block * SEG - TILE : (block + 1) * SEG])
    spans = jnp.concatenate(pieces, 0)
    out = sum(contract(spans, part, 1, 1) for part in split3(band)[::-1])
    return jnp.concatenate([out[b * rows : (b + 1) * rows] for b in range(RAW // SEG)], 1)


def whiten_rows(decimated, keep, table_ref):
    high, low = split2(decimated)
    table_high = table_ref[:SEG, :]
    spectrum = contract(low, table_high, 1, 0) + contract(high, table_ref[SEG:, :], 1, 0)
    spectrum = spectrum + contract(high, table_high, 1, 0)
    real_part, imag_part = spectrum[:, :NBIN], spectrum[:, NBIN:]
    power = real_part * real_part + imag_part * imag_part
    level = jnp.mean(power, -1, keepdims=True)
    scale = keep.astype(jnp.float32) * lax.rsqrt(0.5 * power + 0.5 * level + 1e-05)
    return jnp.concatenate([real_part * scale, imag_part * scale], 1).astype(jnp.bfloat16)


def arrange(piece_ref, spectra_ref):
    members, rows = piece_ref.shape[:2]
    width = rows // WINDOWS
    for pair in range(WINDOWS // 2):
        for quarter in range(4):
            block = piece_ref[:, pair * 2 * width : (pair + 1) * 2 * width, quarter * 128 : (quarter + 1) * 128]
            block = block.astype(jnp.float32)
            for half in range(2):
                turned = block[:, half * width : (half + 1) * width].reshape(members * width, 128).T
                start = (quarter % 2) * 128 * 32 + (quarter // 2) * WINDOWS + pair * 2 + half
                spectra_ref[pl.ds(start, 128, 32), :] = turned


def stack_kernel(same, per_step, *refs):
    if same:
        rows_ref, lag_ref, out_ref, cross_ref, row_spec = refs
    else:
        _, rows_ref, cols_ref, lag_ref, out_ref, cross_ref, row_spec, col_spec = refs

    @pl.when(pl.program_id(0) == 0)
    def _():
        arrange(rows_ref, row_spec)
        if not same:
            arrange(cols_ref, col_spec)

        def one_bin(f, carry):
            start = pl.multiple_of(f * 32, 32)
            left = row_spec[pl.ds(start, 32), :]
            right = left if same else col_spec[pl.ds(start, 32), :]
            turned = jnp.concatenate([right[WINDOWS:], -right[:WINDOWS]], 0)
            both = jnp.concatenate([right, turned], 1).astype(jnp.bfloat16)
            cross = contract(left.astype(jnp.bfloat16), both, 0, 0)
            cross_ref[pl.ds(f, TILE, STRIDE), :] = cross[:, :TILE]
            cross_ref[pl.ds(f + NBIN, TILE, STRIDE), :] = cross[:, TILE:]
            return carry

        lax.fori_loop(0, NBIN, one_bin, 0, unroll=64)

    base = pl.program_id(0) * per_step
    for group in range(per_step // 4):
        picked = []
        for member in range(4):
            start = pl.multiple_of((base + group * 4 + member) * STRIDE, 8)
            picked.append(cross_ref[pl.ds(start, 2 * NBIN), :].astype(jnp.bfloat16))
        stacked = contract(jnp.concatenate(picked, 1), lag_ref[...], 0, 0)
        out_ref[group * 4 : group * 4 + 4] = stacked.reshape(4, TILE, LAGS).astype(jnp.bfloat16)


def stack(gathered, table):
    members = TILE * WINDOWS // gathered.shape[1]
    same = gathered.shape[0] == members
    per_step = 32
    block = (members,) + gathered.shape[1:]
    spectra = pltpu.VMEM((2 * NBIN * WINDOWS, TILE), jnp.float32)
    if same:
        prefetch = []
        sides = [pl.BlockSpec(block, lambda s: (0, 0, 0))]
    else:
        prefetch = [table[lax.axis_index("tiles")]]
        sides = [
            pl.BlockSpec(block, lambda s, entry: (entry[0], 0, 0)),
            pl.BlockSpec(block, lambda s, entry: (entry[1], 0, 0)),
        ]
    return pl.pallas_call(
        functools.partial(stack_kernel, same, per_step),
        out_shape=jax.ShapeDtypeStruct((TILE, TILE, LAGS), jnp.bfloat16),
        grid_spec=pltpu.PrefetchScalarGridSpec(
            num_scalar_prefetch=len(prefetch),
            grid=(TILE // per_step,),
            in_specs=sides + [pl.BlockSpec((2 * NBIN, LAGS), lambda s, *entry: (0, 0))],
            out_specs=pl.BlockSpec((per_step, TILE, LAGS), lambda s, *entry: (s, 0, 0)),
            scratch_shapes=[pltpu.VMEM((TILE * STRIDE, TILE), jnp.float32)] + [spectra] * len(sides),
        ),
        compiler_params=pltpu.CompilerParams(vmem_limit_bytes=60 << 20),
        cost_estimate=pl.CostEstimate(flops=10 << 30, bytes_accessed=12 << 20, transcendentals=0),
    )(*prefetch, *[gathered] * len(sides), lag_table())


def other_core(me):
    return me + 1 - 2 * (me % 2)


def other_chip(me):
    return me + 2 - 4 * ((me // 2) % 2)


def remote(source, target, send, receive, peer):
    return pltpu.make_async_remote_copy(
        src_ref=source,
        dst_ref=target,
        send_sem=send,
        recv_sem=receive,
        device_id={"tiles": peer},
        device_id_type=pl.DeviceIdType.MESH,
    )


def front_kernel(
    devices, raw_hbm, taps_ref, keep_ref, table_hbm, out_ref,
    raw_ref, table_ref, load_sem, sum_buf, part_buf, common_buf, held,
    part_send, part_recv, common_send, common_recv,
    right_send, left_send, chip_send, core_send, held_recv, local_sem,
):
    me = lax.axis_index("tiles")
    channels = raw_ref.shape[1]
    rows = WINDOWS * channels
    barrier = pltpu.get_barrier_semaphore()
    all_owners = devices == WINDOWS

    def greet(k, carry):
        pl.semaphore_signal(
            barrier, inc=1, device_id={"tiles": (me + k) % devices}, device_id_type=pl.DeviceIdType.MESH
        )
        return carry

    lax.fori_loop(1, devices, greet, 0)
    load_raw = pltpu.make_async_copy(raw_hbm, raw_ref, load_sem.at[0])
    load_raw.start()
    load_table = pltpu.make_async_copy(table_hbm, table_ref, load_sem.at[1])
    load_table.start()
    load_raw.wait()
    filtered = filter_rows(raw_ref, taps_ref).reshape(WINDOWS, channels, SEG)
    sum_buf[...] = jnp.sum(filtered, 1, keepdims=True)
    pl.semaphore_wait(barrier, devices - 1)

    def part_copy(owner, slot):
        return remote(sum_buf.at[owner], part_buf.at[slot], part_send.at[owner], part_recv.at[slot], owner)

    def common_copy(owner, peer):
        return remote(common_buf.at[owner], common_buf.at[owner], common_send.at[peer], common_recv.at[owner], peer)

    def send_part(k, carry):
        owner = (me + k) % WINDOWS

        @pl.when(owner != me)
        def _():
            part_copy(owner, me).start()

        return carry

    lax.fori_loop(1 if all_owners else 0, WINDOWS, send_part, 0)

    @pl.when(me < WINDOWS)
    def _():
        part_buf[me] = sum_buf[me]

        def take(k, carry):
            part_copy(me, (me + k) % devices).wait_recv()
            return carry

        lax.fori_loop(1, devices, take, 0)
        common_buf[me] = jnp.sum(part_buf[...], 0)

        def give(k, carry):
            common_copy(me, (me + k) % devices).start()
            return carry

        lax.fori_loop(1, devices, give, 0)

    def take_common(k, carry):
        owner = (me + k) % WINDOWS

        @pl.when(owner != me)
        def _():
            common_copy(owner, me).wait_recv()

        return carry

    lax.fori_loop(1 if all_owners else 0, WINDOWS, take_common, 0)
    common = common_buf[...] / (channels * devices)
    decimated = (filtered - common).reshape(rows, SEG)
    keep = jnp.broadcast_to(keep_ref[...].astype(jnp.float32).T[:, :, None], (WINDOWS, channels, NBIN))
    load_table.wait()
    whitened = whiten_rows(decimated, keep.reshape(rows, NBIN), table_ref)
    held[me] = whitened.reshape(PIECES, rows // PIECES, 2 * NBIN)

    depth = devices // 4
    q, low = me // 4, me % 4
    chip, core = other_chip(me), other_core(me)

    def block_copy(block, piece, send, peer):
        return remote(held.at[block, piece], held.at[block, piece], send, held_recv.at[block, piece], peer)

    def to_right(level, piece):
        return block_copy(4 * level + low, piece, right_send.at[level, piece], (me + 4) % devices)

    def to_left(level, piece):
        return block_copy(4 * level + low, piece, left_send.at[level, piece], (me + devices - 4) % devices)

    def to_chip(level, piece):
        return block_copy(4 * level + low, piece, chip_send.at[level, piece], chip)

    def to_core(block, piece):
        return block_copy(block, piece, core_send.at[block // 2, piece], core)

    def local_copy(block, piece):
        part = rows // PIECES
        return pltpu.make_async_copy(
            held.at[block, piece], out_ref.at[block, pl.ds(piece * part, part)], local_sem.at[block, piece]
        )

    def arrived(block, piece):
        to_core(block, piece).wait_recv()
        local_copy(block, piece).start()

    def line_block(level, piece, forward, go):
        block = 4 * level + low
        arrived(block, piece)

        @pl.when(go)
        def _():
            forward(level, piece).start()

        to_chip(level, piece).start()
        to_core(block, piece).start()

    def chip_block(level, piece):
        block = 4 * level + other_chip(low)
        arrived(block, piece)
        to_core(block, piece).start()

    for piece in range(PIECES):
        @pl.when(q < depth - 1)
        def _():
            to_right(q, piece).start()

        @pl.when(q > 0)
        def _():
            to_left(q, piece).start()

        to_chip(q, piece).start()

    for piece in range(PIECES):
        to_core(me, piece).start()
        local_copy(me, piece).start()

    def step(d, carry):
        for piece in range(PIECES):
            @pl.when(q - d >= 0)
            def _():
                line_block(q - d, piece, to_right, q < depth - 1)

            @pl.when(q + d < depth)
            def _():
                line_block(q + d, piece, to_left, q > 0)

        for piece in range(PIECES):
            @pl.when(d == 1)
            def _():
                chip_block(q, piece)

            @pl.when((d > 1) & (q - d + 1 >= 0))
            def _():
                chip_block(q - d + 1, piece)

            @pl.when((d > 1) & (q + d - 1 < depth))
            def _():
                chip_block(q + d - 1, piece)

        return carry

    lax.fori_loop(1, depth + 1, step, 0)

    def from_core(pair, carry):
        for piece in range(PIECES):
            arrived(2 * pair + core % 2, piece)
        return carry

    lax.fori_loop(0, 2 * depth, from_core, 0)

    def finish(level, carry):
        for piece in range(PIECES):
            @pl.when((level <= q) & (q < depth - 1))
            def _():
                to_right(level, piece).wait_send()

            @pl.when((level >= q) & (q > 0))
            def _():
                to_left(level, piece).wait_send()

            to_chip(level, piece).wait_send()
            to_core(4 * level + low, piece).wait_send()
            to_core(4 * level + other_chip(low), piece).wait_send()
        return carry

    lax.fori_loop(0, depth, finish, 0)

    def drain_part(k, carry):
        owner = (me + k) % WINDOWS

        @pl.when(owner != me)
        def _():
            part_copy(owner, me).wait_send()

        return carry

    lax.fori_loop(1 if all_owners else 0, WINDOWS, drain_part, 0)

    @pl.when(me < WINDOWS)
    def _():
        def drain(k, carry):
            common_copy(me, (me + k) % devices).wait_send()
            return carry

        lax.fori_loop(1, devices, drain, 0)

    def settle(block, carry):
        for piece in range(PIECES):
            local_copy(block, piece).wait()
        return carry

    lax.fori_loop(0, devices, settle, 0)


def front(devices, raw, fir, keep):
    rows = raw.shape[0] * raw.shape[1]
    depth = devices // 4
    dma = pltpu.SemaphoreType.DMA
    vmem = pl.BlockSpec(memory_space=pltpu.VMEM)
    hbm = pl.BlockSpec(memory_space=pl.ANY)
    line = pltpu.VMEM((WINDOWS, 1, SEG), jnp.float32)
    return pl.pallas_call(
        functools.partial(front_kernel, devices),
        out_shape=jax.ShapeDtypeStruct((devices, rows, 2 * NBIN), jnp.bfloat16),
        in_specs=[hbm, vmem, vmem, hbm],
        out_specs=pl.BlockSpec(memory_space=pl.ANY),
        scratch_shapes=[
            pltpu.VMEM(raw.shape, jnp.bfloat16), pltpu.VMEM((2 * SEG, 2 * NBIN), jnp.bfloat16), dma((2,)),
            line, pltpu.VMEM((devices, 1, SEG), jnp.float32), line,
            pltpu.VMEM((devices, PIECES, rows // PIECES, 2 * NBIN), jnp.bfloat16),
            dma((WINDOWS,)), dma((devices,)), dma((devices,)), dma((WINDOWS,)),
            dma((depth, PIECES)), dma((depth, PIECES)), dma((depth, PIECES)), dma((2 * depth, PIECES)),
            dma((devices, PIECES)), dma((devices, PIECES)),
        ],
        compiler_params=pltpu.CompilerParams(
            collective_id=0, has_side_effects=True, vmem_limit_bytes=60 << 20
        ),
    )(raw, fir.reshape(1, TAPS), keep.T, dft_tables())


def local(raw, fir, keep, table):
    gathered = front(lax.axis_size("tiles"), raw, fir, keep)
    return stack(gathered, table)[None]


def solution(mesh):
    placed = (P(None, ("groups", "tiles"), None), P(), P(None, ("groups", "tiles")), P())
    return jax.shard_map(
        local,
        mesh=mesh,
        in_specs=placed,
        out_specs=P(("groups", "tiles"), None, None, None),
        check_vma=False,
    )
```
